32 devices in a mesh: leaf: 4 (over z), rows: 8 (over y, x, core).
Axes of the slice: x: 2, y: 2, z: 4, core: 2. Of those that a mesh axis runs over, the one named last changes fastest.
Arguments:
- rhs: float32 [131072, 256], P(('leaf', 'rows')), may hold values from -6 to 6
- u_basis: float32 [4, 131072, 128], P(None, ('leaf', 'rows')), may hold values from -0.5 to 0.5
- v_basis: float32 [4, 131072, 128], P(None, ('leaf', 'rows')), may hold values from -0.06629126 to 0.06629126
- cap_inv: float32 [15, 256, 256], replicated, may hold values from -0.1125 to 1.1125
Outputs:
- solved: float32 [131072, 256], P(('leaf', 'rows'))
The draws below stay inside these ranges and needn't reach their ends.
All inputs are finite; a program needn't handle non-finite values.
Results may differ from the reference program's by a relative error of at most 0.00012.
Values sent between devices are 32-bit elements; how exact they have to be, the bound alone decides.
A program may use at most 128 MiB of HBM per device.

```python
import jax
import jax.numpy as jnp
from jax import lax

RANK = 128
NRHS = 256
LEVELS = 4
NODES = 15
TOTAL_ROWS = 131072


def draw_v_basis(key, part):
    level = jnp.arange(LEVELS, dtype=jnp.float32)[:, None, None]
    scale = jnp.sqrt(2.0 ** (level + 1.0) / TOTAL_ROWS)
    base = jnp.clip(jax.random.normal(key, (LEVELS, TOTAL_ROWS, RANK), jnp.float32), -6.0, 6.0)
    return base * scale


def draw_cap_inv(key, part):
    order = 2 * RANK
    base = jnp.clip(jax.random.normal(key, (NODES, order, order), jnp.float32), -3.0, 3.0)
    spread = 0.6 / order ** 0.5
    return jnp.eye(order, dtype=jnp.float32)[None] + base * spread


def levels(own_key, dims, split, smallest, top_value):
    gain, own = 1.0, jax.random.fold_in(own_key, 6)
    for axis_at, parts in split:
        steps = jnp.exp(jax.random.uniform(jax.random.fold_in(own, axis_at), (parts,), jnp.float32, smallest / len(split), top_value / len(split)))
        gain = gain * jnp.repeat(steps, dims[axis_at] // parts).reshape([-1 if axis == axis_at else 1 for axis in range(len(dims))])
    return gain


def noise(rng, dims, deviation, bound, split=(), kind=jnp.bfloat16):
    level = levels(rng, dims, split, -0.22, 0.18) if split else 1.0
    values = jax.random.normal(rng, dims, jnp.float32) * deviation * level
    return jnp.minimum(jnp.maximum(values, -bound), bound).astype(kind)


def setup_inputs(seed: int = 0) -> dict:
    keys = jax.random.split(jax.random.key(seed), 5)
    rhs = noise(keys[0], (TOTAL_ROWS, NRHS), 1.0, 6.0, ((0, 32),), jnp.float32)
    u_basis = noise(keys[1], (LEVELS, TOTAL_ROWS, RANK), RANK ** -0.5, 0.5, ((1, 32),), jnp.float32)
    v_basis = draw_v_basis(jax.random.fold_in(keys[4], 71), 0)
    cap_inv = draw_cap_inv(jax.random.fold_in(keys[4], 71), 0)
    return {"rhs": rhs, "u_basis": u_basis, "v_basis": v_basis, "cap_inv": cap_inv}


def reference(rhs, u_basis, v_basis, cap_inv):
    highest = lax.Precision.HIGHEST
    field = rhs
    for level in range(LEVELS):
        kids = 2 ** (level + 1)
        span = TOTAL_ROWS // kids
        shaped = field.reshape(kids, span, NRHS)
        v_rows = v_basis[level].reshape(kids, span, RANK)
        proj = jnp.einsum('csk,csr->ckr', v_rows, shaped, precision=highest)
        stacked = proj.reshape(kids // 2, 2 * RANK, NRHS)
        start = 2 ** level - 1
        caps = cap_inv[start:start + kids // 2]
        coef = jnp.einsum('nij,njr->nir', caps, stacked, precision=highest).reshape(kids, RANK, NRHS)
        u_rows = u_basis[level].reshape(kids, span, RANK)
        field = field - jnp.einsum('csk,ckr->csr', u_rows, coef, precision=highest).reshape(TOTAL_ROWS, NRHS)
    return field
```

```python
import jax
import jax.numpy as jnp
from jax import lax
from jax.experimental import pallas as pl
from jax.experimental.pallas import tpu as pltpu
from jax.sharding import PartitionSpec as P

MESH = pl.DeviceIdType.MESH
CHUNK = 1024
LIMIT = 45 * 2**20
PIECES = (1, 2, 2, 1)
DEPTH = 4
PARTS = 2
PLAN = {(1, 1): (0,), (2, 0): (1,), (2, 1): (0,), (2, 3): (1,), (3, 0): (0,), (3, 1): (2,), (3, 3): (1,)}
TAIL = (3, 0, 2)
F32 = jnp.float32
BF16 = jnp.bfloat16


def split(x):
    high = x.astype(BF16)
    return high, (x - high.astype(F32)).astype(BF16)


def dot(a, b):
    return jnp.dot(a, b, preferred_element_type=F32)


def dot_rows(a, b):
    return lax.dot_general(a, b, (((0,), (0,)), ((), ())), preferred_element_type=F32)


def dot3(a, b):
    ah, al = split(a)
    bh, bl = split(b)
    return dot(ah, bh) + dot(al, bh) + dot(ah, bl)


def make_kernel(levels, rows, rank, width, leaves, lines):
    bits = (leaves * lines).bit_length() - 1
    line_bits = lines.bit_length() - 1
    half = rank // 2
    steps = rows // CHUNK
    tops = [bits - level - 1 for level in range(levels)]
    widths = [width + level * rank for level in range(levels)]

    spread = [bit for bit in (2, 3) if bit < tops[0]]
    others = [bit for bit in range(1, tops[0] + 1) if bit not in spread]

    def masks(chosen):
        return [
            sum(2**bit for k, bit in enumerate(chosen) if index >> k & 1)
            for index in range(1, 2 ** len(chosen))
        ]

    spread_masks, other_masks = masks(spread), masks(others)
    shares = len(spread_masks) + 1
    share = half // shares
    partners = sorted({2**bit for bit in range(bits)} | set(spread_masks) | set(other_masks))
    count = 0
    base = {}
    for level in range(levels):
        if level == 0:
            stages = 3 + 2 * len(spread_masks) + len(other_masks)
            base[level, 0] = count
            count += stages
        else:
            for piece in range(PIECES[level]):
                base[level, piece] = count
                count += tops[level] + 1
            base[level, "pair"] = count
            count += 1
    sems = count

    def kernel(rhs_hbm, u_hbm, v_hbm, cap_hbm, rhs, u, coef, *scratch):
        v, cap = scratch[:2]
        acc = scratch[2 : 2 + levels]
        cur = scratch[2 + levels : 2 + 2 * levels]
        recv = scratch[2 + 2 * levels : 2 + 3 * levels]
        stk = scratch[2 + 3 * levels : 2 + 4 * levels]
        part_in, total_in, in_sem, cap_sem, tx, rx = scratch[2 + 4 * levels :]

        leaf = lax.axis_index("leaf")
        line = lax.axis_index("rows")
        flat = leaf * lines + line
        core = line % 2

        def load(sem, src, dst):
            return pltpu.make_async_copy(src, dst, in_sem.at[sem])

        loads, needs = [], {}
        for step in range(steps):
            at = pl.ds(step * CHUNK, CHUNK)
            needs[0, step] = len(loads)
            loads.append((load(2 * step, rhs_hbm.at[at], rhs.at[at]), load(2 * step + 1, v_hbm.at[0, at], v.at[0, at])))
        for level in range(1, levels + 1):
            for piece in range(PARTS):
                at = pl.ds(piece * (rows // PARTS), rows // PARTS)
                index = len(loads)
                needs[level, piece * (steps // PARTS)] = index
                copies = [load(2 * index, u_hbm.at[level - 1, at], u.at[level - 1, at])]
                if level < levels:
                    copies.append(load(2 * index + 1, v_hbm.at[level, at], v.at[level, at]))
                loads.append(copies)

        def fetch(index):
            if index < len(loads):
                for copy in loads[index]:
                    copy.start()
            elif index == len(loads):
                for copy in cap_in:
                    copy.start()

        def ready(level, step):
            if (level, step) in needs:
                index = needs[level, step]
                for copy in loads[index]:
                    copy.wait()
                fetch(index + DEPTH)

        for index in range(DEPTH):
            fetch(index)
        sides, cap_in = [], []
        for level in range(levels):
            child = flat // (2 ** tops[level])
            side = child % 2
            sides.append(side)
            cap_in.append(
                pltpu.make_async_copy(
                    cap_hbm.at[2**level - 1 + child // 2, pl.ds(pl.multiple_of(side * rank, rank), rank)],
                    cap.at[level],
                    cap_sem.at[level],
                )
            )
        def flip(index, span):
            return index + span - 2 * span * ((index // span) % 2)

        def partner(mask):
            there = {"leaf": leaf, "rows": line}
            for bit in range(bits):
                if mask >> bit & 1:
                    if bit < line_bits:
                        there["rows"] = flip(there["rows"], 2**bit)
                    else:
                        there["leaf"] = flip(there["leaf"], 2 ** (bit - line_bits))
            return there

        barrier = pltpu.get_barrier_semaphore()
        for mask in partners:
            pl.semaphore_signal(barrier, inc=1, device_id=partner(mask), device_id_type=MESH)

        mine = pl.ds(pl.multiple_of(core * half, half), half)
        sent = []

        def send(src, dst, sem, mask):
            copy = pltpu.make_async_remote_copy(
                src_ref=src,
                dst_ref=dst,
                send_sem=tx.at[sem],
                recv_sem=rx.at[sem],
                device_id=partner(mask),
                device_id_type=MESH,
            )
            copy.start()
            sent.append(copy)
            return copy

        def arrived(copies):
            for copy in copies:
                copy.wait_recv()

        def top_level():
            sem = base[0, 0]
            top, side = tops[0], sides[0]
            theirs = pl.ds(pl.multiple_of((1 - core) * half, half), half)
            flying = [send(acc[0].at[theirs], recv[0], sem, 1)]
            sem += 1
            yield
            arrived(flying)
            cur[0][...] = acc[0][mine] + recv[0][...]
            places = [(flat // 2**bit) % 2 for bit in spread]

            def rows_of(index, offset=0):
                place = 0
                for k, bit in enumerate(spread):
                    at = places[k]
                    place = place + 2**k * (1 - at if index >> k & 1 else at)
                return pl.ds(pl.multiple_of(offset + place * share, share), share)

            flying = []
            for index, mask in enumerate(spread_masks):
                flying.append(send(cur[0].at[rows_of(index + 1)], part_in.at[index + 1], sem, mask))
                sem += 1
            yield
            arrived(flying)
            total = cur[0][rows_of(0)]
            for index in range(1, shares):
                total = total + part_in[index]
            part_in[0] = total
            flying = []
            for index, mask in enumerate(other_masks):
                flying.append(send(part_in.at[0], total_in.at[index], sem, mask))
                sem += 1
            yield
            arrived(flying)
            sums = [part_in[0], None]
            for index, mask in enumerate(other_masks):
                k = mask >> top & 1
                sums[k] = total_in[index] if sums[k] is None else sums[k] + total_in[index]
            own = rows_of(0, core * half)
            stk[0][side, own] = sums[0]
            stk[0][1 - side, own] = sums[1]
            flying = []
            for index, mask in enumerate(spread_masks):
                flying.append(send(stk[0].at[:, own], stk[0].at[:, own], sem, mask))
                sem += 1
            yield
            arrived(flying)
            flying = [send(stk[0].at[:, mine], stk[0].at[:, mine], sem, 1)]
            yield
            arrived(flying)

        def sums(level, piece):
            top, sem = tops[level], base[level, piece]
            size = half // PIECES[level]
            here = pl.ds(piece * size, size)
            own = pl.ds(pl.multiple_of(core * half + piece * size, size), size)
            theirs = pl.ds(pl.multiple_of((1 - core) * half + piece * size, size), size)
            flying = send(acc[level].at[theirs], recv[level].at[0, here], sem, 1)
            for at in range(top):
                yield
                flying.wait_recv()
                before = acc[level][own] if at == 0 else cur[level][at - 1, here]
                cur[level][at, here] = before + recv[level][at, here]
                flying = send(cur[level].at[at, here], recv[level].at[at + 1, here], sem + at + 1, 2 ** (at + 1))
            yield
            flying.wait_recv()

        streams = {}

        def begin(level):
            if level == 0:
                streams[level] = [top_level()]
            else:
                streams[level] = [sums(level, piece) for piece in range(PIECES[level])]
            advance(level)

        def advance(level):
            left = []
            for stream in streams[level]:
                try:
                    next(stream)
                    left.append(stream)
                except StopIteration:
                    pass
            streams[level] = left

        def drain(level):
            while streams[level]:
                advance(level)

        pair_in = {}

        def gather(level):
            top, side = tops[level], sides[level]
            pair = jnp.concatenate([cur[level][top - 1], recv[level][top]], axis=0)
            proj = pair[:, :width] - dot3(pair[:, width:], coef[: level * rank])
            stk[level][side, mine] = proj[:half]
            stk[level][1 - side, mine] = proj[half:]
            pair_in[level] = send(stk[level].at[:, mine], stk[level].at[:, mine], base[level, "pair"], 1)

        def finish(level):
            if level:
                pair_in[level].wait_recv()
            stacked = stk[level][...].reshape(2 * rank, width)
            coef[level * rank : (level + 1) * rank] = dot3(cap[level], stacked)

        for level in range(levels):
            for step in range(steps):
                at = pl.ds(step * CHUNK, CHUNK)
                ready(level, step)
                vh, vl = split(v[level, at])
                xh, xl = split(jnp.concatenate([rhs[at]] + [u[k, at] for k in range(level)], axis=1))
                both = dot_rows(jnp.concatenate([vh, vl], axis=1), xh)
                found = both[:rank] + both[rank:] + dot_rows(vh, xl)
                if step:
                    acc[level][...] += found
                else:
                    acc[level][...] = found
                if step == steps - 1:
                    if level == 0:
                        pl.semaphore_wait(barrier, len(partners))
                    begin(level)
                for earlier in PLAN.get((level, step), ()):
                    advance(earlier)

        for step in range(steps):
            ready(levels, step)
        for copy in cap_in:
            copy.wait()
        early = levels // 2

        def subtract(start, stop):
            ch, cl = split(coef[: early * rank])
            for step in range(start, stop):
                at = pl.ds(step * CHUNK, CHUNK)
                uh, ul = split(jnp.concatenate([u[k, at] for k in range(early)], axis=1))
                rhs[at] = rhs[at] - (dot(uh, ch) + dot(uh, cl) + dot(ul, ch))

        for level in TAIL:
            advance(level)
        drain(0)
        finish(0)
        for level in range(1, levels):
            drain(level)
            gather(level)
            if level == early:
                subtract(0, steps // 2)
            if level == levels - 1:
                subtract(steps // 2, steps)
            finish(level)

        for copy in sent:
            copy.wait_send()

    outs = [
        pltpu.VMEM((rows, width), F32),
        pltpu.VMEM((levels, rows, rank), F32),
        pltpu.VMEM((levels * rank, width), F32),
    ]
    scratch_shapes = [
        pltpu.VMEM((levels, rows, rank), F32),
        pltpu.VMEM((levels, rank, 2 * rank), F32),
        *[pltpu.VMEM((rank, w), F32) for w in widths],
        pltpu.VMEM((half, width), F32),
        *[pltpu.VMEM((top, half, w), F32) for top, w in zip(tops[1:], widths[1:])],
        pltpu.VMEM((half, width), F32),
        *[pltpu.VMEM((top + 1, half, w), F32) for top, w in zip(tops[1:], widths[1:])],
        *[pltpu.VMEM((2, rank, width), F32) for _ in widths],
        pltpu.VMEM((shares, share, width), F32),
        pltpu.VMEM((len(other_masks), share, width), F32),
        pltpu.SemaphoreType.DMA((2 * (steps + PARTS * levels),)),
        pltpu.SemaphoreType.DMA((levels,)),
        pltpu.SemaphoreType.DMA((sems,)),
        pltpu.SemaphoreType.DMA((sems,)),
    ]
    return kernel, outs, scratch_shapes


def apply(rhs, u, coef, out_hbm, out, out_sem):
    rows, _ = rhs.shape
    steps = rows // CHUNK
    levels, _, rank = u.shape
    early = levels // 2
    ch, cl = split(coef[early * rank :])

    @pl.loop(0, steps)
    def _(step):
        at = pl.ds(pl.multiple_of(step * CHUNK, CHUNK), CHUNK)
        uh, ul = split(jnp.concatenate([u[k, at] for k in range(early, levels)], axis=1))
        out[at] = rhs[at] - (dot(uh, ch) + dot(uh, cl) + dot(ul, ch))
        pltpu.make_async_copy(out.at[at], out_hbm.at[at], out_sem.at[step]).start()

    for step in range(steps):
        at = pl.ds(step * CHUNK, CHUNK)
        pltpu.make_async_copy(out.at[at], out_hbm.at[at], out_sem.at[step]).wait()


def solution(mesh):
    leaves, lines = mesh.shape["leaf"], mesh.shape["rows"]

    def per_device(rhs, u_basis, v_basis, cap_inv):
        levels, rows, rank = u_basis.shape
        width = rhs.shape[1]
        kernel, outs, scratch_shapes = make_kernel(levels, rows, rank, width, leaves, lines)
        whole = pl.BlockSpec(memory_space=pltpu.VMEM)
        kept = pl.pallas_call(
            kernel,
            out_shape=outs,
            in_specs=[pl.BlockSpec(memory_space=pl.ANY)] * 4,
            out_specs=[whole] * 3,
            scratch_shapes=scratch_shapes,
            compiler_params=pltpu.CompilerParams(
                collective_id=0, has_side_effects=True, vmem_limit_bytes=LIMIT
            ),
        )(rhs, u_basis, v_basis, cap_inv)
        return pl.pallas_call(
            apply,
            out_shape=jax.ShapeDtypeStruct((rows, width), F32),
            in_specs=[whole] * 3,
            out_specs=pl.BlockSpec(memory_space=pl.ANY),
            scratch_shapes=[pltpu.VMEM((rows, width), F32), pltpu.SemaphoreType.DMA((rows // CHUNK,))],
            compiler_params=pltpu.CompilerParams(vmem_limit_bytes=8 * 2**20),
        )(*kept)

    in_specs = (
        P(("leaf", "rows"), None),
        P(None, ("leaf", "rows"), None),
        P(None, ("leaf", "rows"), None),
        P(),
    )
    return jax.shard_map(
        per_device, mesh=mesh, in_specs=in_specs, out_specs=P(("leaf", "rows"), None), check_vma=False
    )
```

```python
import jax
import jax.numpy as jnp
from jax import lax
from jax.experimental import pallas as pl
from jax.experimental.pallas import tpu as pltpu
from jax.sharding import PartitionSpec as P

MESH = pl.DeviceIdType.MESH
CHUNK = 1024
LIMIT = 45 * 2**20
DEPTH = 5
PLAN = {
    (1, 3): (0,),
    (2, 3): (1,),
    (3, 3): (2, 0),
    (4, 3): (3,),
    (5, 3): (4, 1, 2),
    (6, 1): (5,),
    (6, 3): (0, 3),
}
TAIL = (6, 4, 1, 2, 5, 3, 0, 2, 1, 4, "c0", 6, "c1", "c2", "s", "c3")
F32 = jnp.float32
BF16 = jnp.bfloat16


def split(x):
    high = x.astype(BF16)
    return high, (x - high.astype(F32)).astype(BF16)


def dot(a, b):
    return jnp.dot(a, b, preferred_element_type=F32)


def dot_rows(a, b):
    return lax.dot_general(a, b, (((0,), (0,)), ((), ())), preferred_element_type=F32)


def dot3(a, b):
    ah, al = split(a)
    bh, bl = split(b)
    return dot(ah, bh) + dot(al, bh) + dot(ah, bl)


def make_kernel(levels, rows, rank, width, leaves, lines):
    bits = (leaves * lines).bit_length() - 1
    line_bits = lines.bit_length() - 1
    half = rank // 2
    steps = rows // CHUNK
    tops = [bits - level - 1 for level in range(levels)]

    pieces = [(0, 0)]
    for level in range(1, levels):
        pieces += [(level, 0), (level, 1)]
    sizes = [level * rank if inner else width for level, inner in pieces]
    spread = [bit for bit in (2, 3) if bit < tops[0]]
    others = [bit for bit in range(1, tops[0] + 1) if bit not in spread]

    def masks(chosen):
        return [
            sum(2**bit for k, bit in enumerate(chosen) if index >> k & 1)
            for index in range(1, 2 ** len(chosen))
        ]

    spread_masks, other_masks = masks(spread), masks(others)
    shares = len(spread_masks) + 1
    share = half // shares
    partners = sorted({2**bit for bit in range(bits)} | set(spread_masks) | set(other_masks))
    count = 0
    base = []
    for level, inner in pieces:
        base.append(count)
        count += tops[level] + 2 if level else 3 + 2 * len(spread_masks) + len(other_masks)
    sems = count

    def kernel(rhs_hbm, u_hbm, v_hbm, cap_hbm, rhs, u, coef, *scratch):
        v, cap = scratch[:2]
        kinds = len(pieces)
        acc, cur, recv, full = (scratch[2 + k * kinds : 2 + (k + 1) * kinds] for k in range(4))
        part_in, total_in, in_sem, cap_sem, tx, rx = scratch[2 + 4 * kinds :]

        leaf = lax.axis_index("leaf")
        line = lax.axis_index("rows")
        flat = leaf * lines + line
        core = line % 2

        def load(sem, src, dst):
            return pltpu.make_async_copy(src, dst, in_sem.at[sem])

        loads, needs = [], {}
        for step in range(steps):
            at = pl.ds(step * CHUNK, CHUNK)
            needs[0, step] = len(loads)
            loads.append((load(2 * step, rhs_hbm.at[at], rhs.at[at]), load(2 * step + 1, v_hbm.at[0, at], v.at[0, at])))
        def load_whole(key, src, dst):
            needs[key, 0] = len(loads)
            loads.append((load(2 * len(loads), src, dst),))

        for piece, (level, inner) in enumerate(pieces[1:]):
            if inner:
                load_whole(piece + 1, u_hbm.at[level - 1], u.at[level - 1])
            else:
                load_whole(piece + 1, v_hbm.at[level], v.at[level])
        load_whole(len(pieces), u_hbm.at[levels - 1], u.at[levels - 1])

        def fetch(index):
            if index < len(loads):
                for copy in loads[index]:
                    copy.start()
            elif index == len(loads):
                for copy in cap_in:
                    copy.start()

        def ready(piece, step):
            if (piece, step) in needs:
                index = needs[piece, step]
                for copy in loads[index]:
                    copy.wait()
                fetch(index + DEPTH)

        for index in range(DEPTH):
            fetch(index)
        sides, cap_in = [], []
        for level in range(levels):
            child = flat // (2 ** tops[level])
            side = child % 2
            sides.append(side)
            cap_in.append(
                pltpu.make_async_copy(
                    cap_hbm.at[2**level - 1 + child // 2, pl.ds(pl.multiple_of(side * rank, rank), rank)],
                    cap.at[level],
                    cap_sem.at[level],
                )
            )
        def flip(index, span):
            return index + span - 2 * span * ((index // span) % 2)

        def partner(mask):
            there = {"leaf": leaf, "rows": line}
            for bit in range(bits):
                if mask >> bit & 1:
                    if bit < line_bits:
                        there["rows"] = flip(there["rows"], 2**bit)
                    else:
                        there["leaf"] = flip(there["leaf"], 2 ** (bit - line_bits))
            return there

        barrier = pltpu.get_barrier_semaphore()
        for mask in partners:
            pl.semaphore_signal(barrier, inc=1, device_id=partner(mask), device_id_type=MESH)

        mine = pl.ds(pl.multiple_of(core * half, half), half)
        sent = []

        def send(src, dst, sem, mask):
            copy = pltpu.make_async_remote_copy(
                src_ref=src,
                dst_ref=dst,
                send_sem=tx.at[sem],
                recv_sem=rx.at[sem],
                device_id=partner(mask),
                device_id_type=MESH,
            )
            copy.start()
            sent.append(copy)
            return copy

        def arrived(copies):
            for copy in copies:
                copy.wait_recv()

        def top_level():
            sem = base[0]
            top, side = tops[0], sides[0]
            theirs = pl.ds(pl.multiple_of((1 - core) * half, half), half)
            flying = [send(acc[0].at[theirs], recv[0].at[0], sem, 1)]
            sem += 1
            yield
            arrived(flying)
            cur[0][0] = acc[0][mine] + recv[0][0]
            places = [(flat // 2**bit) % 2 for bit in spread]

            def rows_of(index, offset=0):
                place = 0
                for k, bit in enumerate(spread):
                    at = places[k]
                    place = place + 2**k * (1 - at if index >> k & 1 else at)
                return pl.ds(pl.multiple_of(offset + place * share, share), share)

            flying = []
            for index, mask in enumerate(spread_masks):
                flying.append(send(cur[0].at[0, rows_of(index + 1)], part_in.at[index + 1], sem, mask))
                sem += 1
            yield
            arrived(flying)
            total = cur[0][0, rows_of(0)]
            for index in range(1, shares):
                total = total + part_in[index]
            part_in[0] = total
            flying = []
            for index, mask in enumerate(other_masks):
                flying.append(send(part_in.at[0], total_in.at[index], sem, mask))
                sem += 1
            yield
            arrived(flying)
            sums = [part_in[0], None]
            for index, mask in enumerate(other_masks):
                k = mask >> top & 1
                sums[k] = total_in[index] if sums[k] is None else sums[k] + total_in[index]
            own = rows_of(0, core * half)
            full[0][side, own] = sums[0]
            full[0][1 - side, own] = sums[1]
            flying = []
            for index, mask in enumerate(spread_masks):
                flying.append(send(full[0].at[:, own], full[0].at[:, own], sem, mask))
                sem += 1
            yield
            arrived(flying)
            flying = [send(full[0].at[:, mine], full[0].at[:, mine], sem, 1)]
            yield
            arrived(flying)

        def sums(piece):
            level = pieces[piece][0]
            top, sem, side = tops[level], base[piece], sides[level]
            theirs = pl.ds(pl.multiple_of((1 - core) * half, half), half)
            flying = send(acc[piece].at[theirs], recv[piece].at[0], sem, 1)
            for at in range(top):
                yield
                flying.wait_recv()
                before = acc[piece][mine] if at == 0 else cur[piece][at - 1]
                cur[piece][at] = before + recv[piece][at]
                flying = send(cur[piece].at[at], recv[piece].at[at + 1], sem + at + 1, 2 ** (at + 1))
            yield
            flying.wait_recv()
            full[piece][side, mine] = cur[piece][top - 1]
            full[piece][1 - side, mine] = recv[piece][top]
            flying = send(full[piece].at[:, mine], full[piece].at[:, mine], sem + top + 1, 1)
            yield
            flying.wait_recv()

        streams = {}

        def advance(piece):
            if streams.get(piece):
                try:
                    next(streams[piece])
                except StopIteration:
                    streams[piece] = None

        def begin(piece):
            streams[piece] = sums(piece) if piece else top_level()
            advance(piece)

        def chain(level):
            first = 2 * level - 1 if level else 0
            for piece in (first, first + 1) if level else (0,):
                while streams.get(piece):
                    advance(piece)
            proj = full[first][...].reshape(2 * rank, width)
            if level:
                inner = full[first + 1][...].reshape(2 * rank, level * rank)
                proj = proj - dot3(inner, coef[: level * rank])
            coef[level * rank : (level + 1) * rank] = dot3(cap[level], proj)

        def columns(blocks, at, vh, vl):
            found = []
            both_v = jnp.concatenate([vh, vl], axis=1)
            for k in range(0, len(blocks), 2):
                pair = blocks[k : k + 2]
                xh, xl = split(jnp.concatenate([block[at] for block in pair], axis=1))
                if len(pair) == 1:
                    both = dot_rows(both_v, jnp.concatenate([xh, xl], axis=1))
                    found.append(both[:rank, :rank] + both[rank:, :rank] + both[:rank, rank:])
                else:
                    both = dot_rows(both_v, xh)
                    found.append(both[:rank] + both[rank:] + dot_rows(vh, xl))
            return found[0] if len(found) == 1 else jnp.concatenate(found, axis=1)

        for piece, (level, inner) in enumerate(pieces):
            if inner:
                blocks = [u.at[k] for k in range(level)]
            else:
                blocks = [rhs.at[:, k : k + rank] for k in range(0, width, rank)]
            for step in range(steps):
                at = pl.ds(step * CHUNK, CHUNK)
                ready(piece, step)
                vh, vl = split(v[level, at])
                found = columns(blocks, at, vh, vl)
                if step:
                    acc[piece][...] += found
                else:
                    acc[piece][...] = found
                if step == steps - 1:
                    if piece == 0:
                        pl.semaphore_wait(barrier, len(partners))
                    begin(piece)
                for earlier in PLAN.get((piece, step), ()):
                    advance(earlier)

        for step in range(steps):
            ready(len(pieces), step)
        for copy in cap_in:
            copy.wait()
        early = levels // 2

        def subtract(start, stop):
            ch, cl = split(coef[: early * rank])
            for step in range(start, stop):
                at = pl.ds(step * CHUNK, CHUNK)
                uh, ul = split(jnp.concatenate([u[k, at] for k in range(early)], axis=1))
                rhs[at] = rhs[at] - (dot(uh, ch) + dot(uh, cl) + dot(ul, ch))

        for event in TAIL:
            if event == "s":
                subtract(0, steps)
            elif event in ("c0", "c1", "c2", "c3"):
                chain(int(event[1]))
            else:
                advance(event)

        for copy in sent:
            copy.wait_send()

    outs = [
        pltpu.VMEM((rows, width), F32),
        pltpu.VMEM((levels, rows, rank), F32),
        pltpu.VMEM((levels * rank, width), F32),
    ]
    scratch_shapes = [
        pltpu.VMEM((levels, rows, rank), F32),
        pltpu.VMEM((levels, rank, 2 * rank), F32),
        *[pltpu.VMEM((rank, size), F32) for size in sizes],
        *[pltpu.VMEM((max(1, tops[level]) if level else 1, half, size), F32) for (level, _), size in zip(pieces, sizes)],
        *[pltpu.VMEM((tops[level] + 1 if level else 1, half, size), F32) for (level, _), size in zip(pieces, sizes)],
        *[pltpu.VMEM((2, rank, size), F32) for size in sizes],
        pltpu.VMEM((shares, share, width), F32),
        pltpu.VMEM((len(other_masks), share, width), F32),
        pltpu.SemaphoreType.DMA((2 * (steps + 2 * levels),)),
        pltpu.SemaphoreType.DMA((levels,)),
        pltpu.SemaphoreType.DMA((sems,)),
        pltpu.SemaphoreType.DMA((sems,)),
    ]
    return kernel, outs, scratch_shapes


def apply(rhs, u, coef, out_hbm, out, out_sem):
    rows, _ = rhs.shape
    steps = rows // CHUNK
    levels, _, rank = u.shape
    early = levels // 2
    ch, cl = split(coef[early * rank :])

    @pl.loop(0, steps)
    def _(step):
        at = pl.ds(pl.multiple_of(step * CHUNK, CHUNK), CHUNK)
        uh, ul = split(jnp.concatenate([u[k, at] for k in range(early, levels)], axis=1))
        out[at] = rhs[at] - (dot(uh, ch) + dot(uh, cl) + dot(ul, ch))
        pltpu.make_async_copy(out.at[at], out_hbm.at[at], out_sem.at[step]).start()

    for step in range(steps):
        at = pl.ds(step * CHUNK, CHUNK)
        pltpu.make_async_copy(out.at[at], out_hbm.at[at], out_sem.at[step]).wait()


def solution(mesh):
    leaves, lines = mesh.shape["leaf"], mesh.shape["rows"]

    def per_device(rhs, u_basis, v_basis, cap_inv):
        levels, rows, rank = u_basis.shape
        width = rhs.shape[1]
        kernel, outs, scratch_shapes = make_kernel(levels, rows, rank, width, leaves, lines)
        whole = pl.BlockSpec(memory_space=pltpu.VMEM)
        kept = pl.pallas_call(
            kernel,
            out_shape=outs,
            in_specs=[pl.BlockSpec(memory_space=pl.ANY)] * 4,
            out_specs=[whole] * 3,
            scratch_shapes=scratch_shapes,
            compiler_params=pltpu.CompilerParams(
                collective_id=0, has_side_effects=True, vmem_limit_bytes=LIMIT
            ),
        )(rhs, u_basis, v_basis, cap_inv)
        return pl.pallas_call(
            apply,
            out_shape=jax.ShapeDtypeStruct((rows, width), F32),
            in_specs=[whole] * 3,
            out_specs=pl.BlockSpec(memory_space=pl.ANY),
            scratch_shapes=[pltpu.VMEM((rows, width), F32), pltpu.SemaphoreType.DMA((rows // CHUNK,))],
            compiler_params=pltpu.CompilerParams(vmem_limit_bytes=8 * 2**20),
        )(*kept)

    in_specs = (
        P(("leaf", "rows"), None),
        P(None, ("leaf", "rows"), None),
        P(None, ("leaf", "rows"), None),
        P(),
    )
    return jax.shard_map(
        per_device, mesh=mesh, in_specs=in_specs, out_specs=P(("leaf", "rows"), None), check_vma=False
    )
```

```python
import jax
import jax.numpy as jnp
from jax import lax
from jax.experimental import pallas as pl
from jax.experimental.pallas import tpu as pltpu
from jax.sharding import PartitionSpec as P

MESH = pl.DeviceIdType.MESH
CHUNK = 1024
LIMIT = 45 * 2**20
DEPTH = 5
EARLY = 2
MERGED = ()
PLAN = {
    (1, 3): (0,),
    (2, 3): (1,),
    (3, 3): (2, 0),
    (4, 3): (3,),
    (5, 3): (4, 1, 2),
    (6, 1): (5,),
    (6, 3): (0, 3),
}
TAIL = (6, 4, 1, 2, 5, 3, 0, 2, 1, 4, 6, 0, "c0", "c1", "c2", "s", "c3")
ENDS = (512, 1024, 1024, 1024, 256, 256)
F32 = jnp.float32
BF16 = jnp.bfloat16


def split(x):
    high = x.astype(BF16)
    return high, (x - high.astype(F32)).astype(BF16)


def dot(a, b):
    return jnp.dot(a, b, preferred_element_type=F32)


def dot_rows(a, b):
    return lax.dot_general(a, b, (((0,), (0,)), ((), ())), preferred_element_type=F32)


def dot3(a, b):
    ah, al = split(a)
    bh, bl = split(b)
    return dot(ah, bh) + dot(al, bh) + dot(ah, bl)


def make_kernel(levels, rows, rank, width, leaves, lines):
    bits = (leaves * lines).bit_length() - 1
    line_bits = lines.bit_length() - 1
    half = rank // 2
    steps = rows // CHUNK
    tops = [bits - level - 1 for level in range(levels)]

    pieces = [(0, 0)]
    for level in range(1, levels):
        pieces += [(level, 0), (level, 1)]
    owner, offset, streams_of = [0], [0], [(0, width)]
    for piece, (level, inner) in enumerate(pieces[1:], 1):
        size = level * rank if inner else width
        if inner and level in MERGED:
            owner.append(owner[-1])
            offset.append(streams_of[-1][1])
            streams_of[-1] = (level, streams_of[-1][1] + size)
        else:
            owner.append(len(streams_of))
            offset.append(0)
            streams_of.append((level, size))
    last = {stream: piece for piece, stream in enumerate(owner)}
    spread = [bit for bit in (2, 3) if bit < tops[0]]
    others = [bit for bit in range(1, tops[0] + 1) if bit not in spread]

    def masks(chosen):
        return [
            sum(2**bit for k, bit in enumerate(chosen) if index >> k & 1)
            for index in range(1, 2 ** len(chosen))
        ]

    spread_masks, other_masks = masks(spread), masks(others)
    shares = len(spread_masks) + 1
    share = half // shares
    partners = sorted({2**bit for bit in range(bits)} | set(spread_masks) | set(other_masks))
    count = 0
    base = []
    for level, _ in streams_of:
        base.append(count)
        count += tops[level] + 2 if level else 3 + 2 * len(spread_masks) + len(other_masks)
    sems = count

    def kernel(rhs_hbm, u_hbm, v_hbm, cap_hbm, rhs, u, coef, *scratch):
        v, cap = scratch[:2]
        kinds = len(streams_of)
        acc, cur, recv, full = (scratch[2 + k * kinds : 2 + (k + 1) * kinds] for k in range(4))
        part_in, total_in, in_sem, cap_sem, tx, rx = scratch[2 + 4 * kinds :]

        leaf = lax.axis_index("leaf")
        line = lax.axis_index("rows")
        flat = leaf * lines + line
        core = line % 2

        def load(sem, src, dst):
            return pltpu.make_async_copy(src, dst, in_sem.at[sem])

        loads, needs = [], {}
        for step in range(steps):
            at = pl.ds(step * CHUNK, CHUNK)
            needs[0, step] = len(loads)
            loads.append((load(2 * step, rhs_hbm.at[at], rhs.at[at]), load(2 * step + 1, v_hbm.at[0, at], v.at[0, at])))
        def load_whole(key, src, dst):
            needs[key, 0] = len(loads)
            loads.append((load(2 * len(loads), src, dst),))

        for piece, (level, inner) in enumerate(pieces[1:]):
            if inner:
                load_whole(piece + 1, u_hbm.at[level - 1], u.at[level - 1])
            else:
                load_whole(piece + 1, v_hbm.at[level], v.at[level])
        load_whole(len(pieces), u_hbm.at[levels - 1], u.at[levels - 1])

        def fetch(index):
            if index < len(loads):
                for copy in loads[index]:
                    copy.start()
            elif index == len(loads):
                for copy in cap_in:
                    copy.start()

        def ready(piece, step):
            if (piece, step) in needs:
                index = needs[piece, step]
                for copy in loads[index]:
                    copy.wait()
                fetch(index + DEPTH)

        for index in range(DEPTH):
            fetch(index)
        sides, cap_in = [], []
        for level in range(levels):
            child = flat // (2 ** tops[level])
            side = child % 2
            sides.append(side)
            cap_in.append(
                pltpu.make_async_copy(
                    cap_hbm.at[2**level - 1 + child // 2, pl.ds(pl.multiple_of(side * rank, rank), rank)],
                    cap.at[level],
                    cap_sem.at[level],
                )
            )
        def flip(index, span):
            return index + span - 2 * span * ((index // span) % 2)

        known = {}

        def partner(mask):
            if mask in known:
                return known[mask]
            there = {"leaf": leaf, "rows": line}
            for bit in range(bits):
                if mask >> bit & 1:
                    if bit < line_bits:
                        there["rows"] = flip(there["rows"], 2**bit)
                    else:
                        there["leaf"] = flip(there["leaf"], 2 ** (bit - line_bits))
            known[mask] = there
            return there

        barrier = pltpu.get_barrier_semaphore()
        for mask in partners:
            pl.semaphore_signal(barrier, inc=1, device_id=partner(mask), device_id_type=MESH)

        mine = pl.ds(pl.multiple_of(core * half, half), half)
        sent = []

        def send(src, dst, sem, mask):
            copy = pltpu.make_async_remote_copy(
                src_ref=src,
                dst_ref=dst,
                send_sem=tx.at[sem],
                recv_sem=rx.at[sem],
                device_id=partner(mask),
                device_id_type=MESH,
            )
            copy.start()
            sent.append(copy)
            return copy

        def arrived(copies):
            for copy in copies:
                copy.wait_recv()

        def top_level():
            sem = base[0]
            top, side = tops[0], sides[0]
            theirs = pl.ds(pl.multiple_of((1 - core) * half, half), half)
            flying = [send(acc[0].at[theirs], recv[0].at[0], sem, 1)]
            sem += 1
            yield
            arrived(flying)
            cur[0][0] = acc[0][mine] + recv[0][0]
            places = [(flat // 2**bit) % 2 for bit in spread]

            def rows_of(index, offset=0):
                place = 0
                for k, bit in enumerate(spread):
                    at = places[k]
                    place = place + 2**k * (1 - at if index >> k & 1 else at)
                return pl.ds(pl.multiple_of(offset + place * share, share), share)

            flying = []
            for index, mask in enumerate(spread_masks):
                flying.append(send(cur[0].at[0, rows_of(index + 1)], part_in.at[index + 1], sem, mask))
                sem += 1
            yield
            arrived(flying)
            total = cur[0][0, rows_of(0)]
            for index in range(1, shares):
                total = total + part_in[index]
            part_in[0] = total
            flying = []
            for index, mask in enumerate(other_masks):
                flying.append(send(part_in.at[0], total_in.at[index], sem, mask))
                sem += 1
            yield
            arrived(flying)
            sums = [part_in[0], None]
            for index, mask in enumerate(other_masks):
                k = mask >> top & 1
                sums[k] = total_in[index] if sums[k] is None else sums[k] + total_in[index]
            own = rows_of(0, core * half)
            full[0][side, own] = sums[0]
            full[0][1 - side, own] = sums[1]
            flying = []
            for index, mask in enumerate(spread_masks):
                flying.append(send(full[0].at[:, own], full[0].at[:, own], sem, mask))
                sem += 1
            yield
            arrived(flying)
            flying = [send(full[0].at[:, mine], full[0].at[:, mine], sem, 1)]
            yield
            arrived(flying)

        def sums(piece):
            level = streams_of[piece][0]
            top, sem, side = tops[level], base[piece], sides[level]
            theirs = pl.ds(pl.multiple_of((1 - core) * half, half), half)
            shared = full[piece]
            flying = send(acc[piece].at[theirs], recv[piece].at[0], sem, 1)
            for at in range(top):
                yield
                flying.wait_recv()
                found = (acc[piece][mine] if at == 0 else cur[piece][at - 1]) + recv[piece][at]
                if at < top - 1:
                    cur[piece][at] = found
                    flying = send(cur[piece].at[at], recv[piece].at[at + 1], sem + at + 1, 2 ** (at + 1))
                else:
                    shared[side, mine] = found
                    flying = send(shared.at[side, mine], shared.at[side, mine], sem + top, 2**top)
            yield
            flying.wait_recv()
            flying = send(shared.at[:, mine], shared.at[:, mine], sem + top + 1, 1)
            yield
            flying.wait_recv()

        streams = {}

        def advance(piece):
            if streams.get(piece):
                try:
                    next(streams[piece])
                except StopIteration:
                    streams[piece] = None

        def begin(piece):
            streams[piece] = sums(piece) if piece else top_level()
            advance(piece)

        def chain(level):
            first = 2 * level - 1 if level else 0
            for piece in (first, first + 1) if level else (0,):
                while streams.get(owner[piece]):
                    advance(owner[piece])
            found = full[owner[first]][...].reshape(2 * rank, streams_of[owner[first]][1])
            proj = found[:, :width]
            if level:
                at = offset[first + 1]
                inner = found[:, at:] if at else full[owner[first + 1]][...].reshape(2 * rank, level * rank)
                proj = proj - dot3(inner, coef[: level * rank])
            coef[level * rank : (level + 1) * rank] = dot3(cap[level], proj)

        def columns(blocks, at, vh, vl):
            found = []
            both_v = jnp.concatenate([vh, vl], axis=1)
            for k in range(0, len(blocks), 2):
                pair = blocks[k : k + 2]
                xh, xl = split(jnp.concatenate([block[at] for block in pair], axis=1))
                if len(pair) == 1:
                    both = dot_rows(both_v, jnp.concatenate([xh, xl], axis=1))
                    found.append(both[:rank, :rank] + both[rank:, :rank] + both[:rank, rank:])
                else:
                    both = dot_rows(both_v, xh)
                    found.append(both[:rank] + both[rank:] + dot_rows(vh, xl))
            return found[0] if len(found) == 1 else jnp.concatenate(found, axis=1)

        for piece, (level, inner) in enumerate(pieces):
            if inner:
                blocks = [u.at[k] for k in range(level)]
            else:
                blocks = [rhs.at[:, k : k + rank] for k in range(0, width, rank)]
            for step in range(steps):
                at = pl.ds(step * CHUNK, CHUNK)
                ready(piece, step)
                vh, vl = split(v[level, at])
                found = columns(blocks, at, vh, vl)
                into = slice(offset[piece], offset[piece] + found.shape[1])
                if step:
                    acc[owner[piece]][:, into] += found
                else:
                    acc[owner[piece]][:, into] = found
                if step == steps - 1 and last[owner[piece]] == piece:
                    if piece == 0:
                        pl.semaphore_wait(barrier, len(partners))
                    begin(owner[piece])
                for earlier in PLAN.get((piece, step), ()):
                    advance(earlier)

        for step in range(steps):
            ready(len(pieces), step)
        for copy in cap_in:
            copy.wait()

        def subtract(first, stop):
            ch, cl = split(coef[first * rank : stop * rank])
            ends = jnp.concatenate([ch, ch], axis=0)
            for step in range(steps):
                at = pl.ds(step * CHUNK, CHUNK)
                uh, ul = split(jnp.concatenate([u[k, at] for k in range(first, stop)], axis=1))
                if stop - first == 1:
                    rhs[at] = rhs[at] - (dot(jnp.concatenate([uh, ul], axis=1), ends) + dot(uh, cl))
                else:
                    rhs[at] = rhs[at] - (dot(uh, ch) + dot(uh, cl) + dot(ul, ch))

        for event in TAIL:
            if event == "s":
                subtract(0, EARLY)
            elif event in ("s0", "s1", "s2"):
                subtract(int(event[1]), int(event[1]) + 1)
            elif event in ("c0", "c1", "c2", "c3"):
                chain(int(event[1]))
            else:
                advance(event)

        for copy in sent:
            copy.wait_send()

    outs = [
        pltpu.VMEM((rows, width), F32),
        pltpu.VMEM((levels, rows, rank), F32),
        pltpu.VMEM((levels * rank, width), F32),
    ]
    scratch_shapes = [
        pltpu.VMEM((levels, rows, rank), F32),
        pltpu.VMEM((levels, rank, 2 * rank), F32),
        *[pltpu.VMEM((rank, size), F32) for _, size in streams_of],
        *[pltpu.VMEM((max(tops[level] - 1, 1) if level else 1, half, size), F32) for level, size in streams_of],
        *[pltpu.VMEM((tops[level] if level else 1, half, size), F32) for level, size in streams_of],
        *[pltpu.VMEM((2, rank, size), F32) for _, size in streams_of],
        pltpu.VMEM((shares, share, width), F32),
        pltpu.VMEM((len(other_masks), share, width), F32),
        pltpu.SemaphoreType.DMA((2 * (steps + 2 * levels),)),
        pltpu.SemaphoreType.DMA((levels,)),
        pltpu.SemaphoreType.DMA((sems,)),
        pltpu.SemaphoreType.DMA((sems,)),
    ]
    return kernel, outs, scratch_shapes


def parts_of(rows):
    sizes = [part * rows // sum(ENDS) for part in ENDS]
    assert sum(sizes) == rows
    return sizes


def apply(rhs, u, coef, out_hbm, out, out_sem):
    rows, _ = rhs.shape
    levels, _, rank = u.shape
    early = EARLY
    ch, cl = split(coef[early * rank :])

    copies, start = [], 0
    for size in parts_of(rows):
        at = pl.ds(start, size)
        uh, ul = split(jnp.concatenate([u[k, at] for k in range(early, levels)], axis=1))
        out[at] = rhs[at] - (dot(uh, ch) + dot(uh, cl) + dot(ul, ch))
        copies.append(pltpu.make_async_copy(out.at[at], out_hbm.at[at], out_sem.at[len(copies)]))
        copies[-1].start()
        start += size
    for copy in copies:
        copy.wait()


def solution(mesh):
    leaves, lines = mesh.shape["leaf"], mesh.shape["rows"]

    def per_device(rhs, u_basis, v_basis, cap_inv):
        levels, rows, rank = u_basis.shape
        width = rhs.shape[1]
        kernel, outs, scratch_shapes = make_kernel(levels, rows, rank, width, leaves, lines)
        whole = pl.BlockSpec(memory_space=pltpu.VMEM)
        kept = pl.pallas_call(
            kernel,
            out_shape=outs,
            in_specs=[pl.BlockSpec(memory_space=pl.ANY)] * 4,
            out_specs=[whole] * 3,
            scratch_shapes=scratch_shapes,
            compiler_params=pltpu.CompilerParams(
                collective_id=0, has_side_effects=True, vmem_limit_bytes=LIMIT
            ),
        )(rhs, u_basis, v_basis, cap_inv)
        return pl.pallas_call(
            apply,
            out_shape=jax.ShapeDtypeStruct((rows, width), F32),
            in_specs=[whole] * 3,
            out_specs=pl.BlockSpec(memory_space=pl.ANY),
            scratch_shapes=[pltpu.VMEM((rows, width), F32), pltpu.SemaphoreType.DMA((len(ENDS),))],
            compiler_params=pltpu.CompilerParams(vmem_limit_bytes=8 * 2**20),
        )(*kept)

    in_specs = (
        P(("leaf", "rows"), None),
        P(None, ("leaf", "rows"), None),
        P(None, ("leaf", "rows"), None),
        P(),
    )
    return jax.shard_map(
        per_device, mesh=mesh, in_specs=in_specs, out_specs=P(("leaf", "rows"), None), check_vma=False
    )
```
